32 devices in a mesh: prow: 4 (over y, x), pcol: 8 (over z, core).
Axes of the slice: x: 2, y: 2, z: 4, core: 2. Of those that a mesh axis runs over, the one named last changes fastest.
Arguments:
- schur: float32 [4, 4, 128, 2, 8, 128], P(None, 'prow', None, None, 'pcol'), may hold values from -0.125 to 0.125
- panel_inverse: float32 [2, 8, 128, 2, 4, 128], P(None, 'pcol', None, None, 'prow'), may hold values from -0.1875 to 0.1875
- coupling: float32 [4, 4, 128, 256], P(None, 'prow'), may hold values from -6 to 6
- zslab: float32 [4, 4, 128, 2, 8, 128], P(None, 'prow', None, None, 'pcol')
- targets: int32 [128], replicated, may hold values from 0 to 254
- pair_flags: int32 [128], replicated, may hold values 0 or 1
Outputs:
- eigenvectors: float32 [4, 4, 128, 128], P(None, 'prow', 'pcol')
The draws below stay inside these ranges and needn't reach their ends.
All inputs are finite; a program needn't handle non-finite values.
Results may differ from the reference program's by a relative error of at most 0.0001.
Values sent between devices are 32-bit elements; how exact they have to be, the bound alone decides.
A program may use at most 64 MiB of HBM per device.

```python
import math
import jax
import jax.numpy as jnp
from jax import lax

BS = 128
NRHS = 128
WIN = 256
CBLK = 2
ZRB = 4
PW = 1024
RP = 2
K = 2048
RBLK = 4
ZROWS = 2048
N_PROW = 4
N_PCOL = 8


def draw_zslab(key, part):
    normal_key, scale_key = jax.random.split(jax.random.fold_in(key, 17))
    full_shape = (ZRB, N_PROW, BS, CBLK, N_PCOL, BS)
    entries = jax.random.normal(normal_key, full_shape, jnp.float32)
    spread = jax.random.uniform(scale_key, (ZRB, N_PROW, BS), jnp.float32)
    prow_frac = jnp.arange(N_PROW, dtype=jnp.float32) / (N_PROW - 1)
    share_frac = (jnp.arange(BS, dtype=jnp.int32) // (BS // N_PCOL)).astype(jnp.float32) / (N_PCOL - 1)
    exponent = 0.25 * prow_frac[None, :, None] + 0.25 * share_frac[None, None, :] + 0.5 * spread
    row_scale = jnp.power(10.0, exponent) / math.sqrt(K)
    return entries * row_scale[:, :, :, None, None, None]


def plant(array, stream_key, least, high):
    shape = array.shape
    place = [jax.random.randint(jax.random.fold_in(stream_key, axis), (), 0, shape[axis]) for axis in range(len(shape))]
    array = array.at[tuple(place)].set(least)
    longest = shape.index(max(shape))
    place[longest] = (place[longest] + 1) % shape[longest]
    return array.at[tuple(place)].set(high)


def block_scale(own_key, shape, cuts, low, top_value):
    def one(axis_at, shards_of):
        heights = jax.random.uniform(jax.random.fold_in(jax.random.fold_in(own_key, 6), axis_at), (shards_of,), jnp.float32, low / len(cuts), top_value / len(cuts))
        return jnp.repeat(jnp.exp(heights), shape[axis_at] // shards_of).reshape((-1,) + (1,) * (len(shape) - axis_at - 1))

    loudness = one(*cuts[0])
    for cut in cuts[1:]:
        loudness = loudness * one(*cut)
    return loudness


def normal_values(stream_key, extent, scale, reach, cuts=(), kind=jnp.bfloat16):
    result = jax.random.normal(stream_key, extent, jnp.float32) * scale
    if len(cuts) > 0:
        result = block_scale(stream_key, extent, cuts, -0.22, 0.18) * result
    return jnp.clip(result, min=-reach, max=reach).astype(kind)


def setup_inputs(seed: int = 0) -> dict:
    key_list = jax.random.split(jax.random.key(seed), 7)
    schur = normal_values(key_list[0], (RBLK, N_PROW, BS, CBLK, N_PCOL, BS), K ** -0.5, 0.125, ((1, 4), (4, 8)), jnp.float32)
    panel_inverse = normal_values(key_list[1], (CBLK, N_PCOL, BS, RP, N_PROW, BS), PW ** -0.5, 0.1875, ((1, 8), (4, 4)), jnp.float32)
    coupling = normal_values(key_list[2], (RBLK, N_PROW, BS, WIN), 1.0, 6.0, ((1, 4),), jnp.float32)
    zslab = draw_zslab(jax.random.fold_in(key_list[6], 71), 0)
    targets = plant(jax.random.randint(key_list[4], (NRHS,), 0, WIN - 1), jax.random.fold_in(key_list[4], 1), 0, (WIN - 1) - 1).astype(jnp.int32)
    pair_flags = plant((jax.random.randint(key_list[5], (NRHS,), 0, 2) < 1).astype(jnp.int32), jax.random.fold_in(key_list[5], 1), 0, 1)
    return dict(schur=schur, panel_inverse=panel_inverse, coupling=coupling, zslab=zslab, targets=targets, pair_flags=pair_flags)


EPSILON = 1e-06

def reference(schur, panel_inverse, coupling, zslab, targets, pair_flags):
    triangle = schur.reshape(K, K)
    columns = jnp.arange(WIN, dtype=jnp.int32)[:, None]
    selection = (columns == targets[None, :]).astype(jnp.float32) + pair_flags[None, :].astype(jnp.float32) * (columns == targets[None, :] + 1).astype(jnp.float32)
    right_side = -jnp.dot(coupling.reshape(K, WIN), selection, precision=lax.Precision.HIGHEST)
    inverse = panel_inverse.reshape(CBLK, PW, PW)
    pieces = [None] * CBLK
    for panel_index in reversed(range(CBLK)):
        residual = right_side[panel_index * PW:(panel_index + 1) * PW]
        if panel_index < CBLK - 1:
            later_rows = jnp.concatenate(pieces[panel_index + 1:], axis=0)
            residual = residual - jnp.dot(triangle[panel_index * PW:(panel_index + 1) * PW, (panel_index + 1) * PW:], later_rows, precision=lax.Precision.HIGHEST)
        pieces[panel_index] = jnp.dot(inverse[panel_index], residual, precision=lax.Precision.HIGHEST)
    vectors = jnp.concatenate(pieces, axis=0)
    transformed = jnp.dot(zslab.reshape(ZROWS, K), vectors, precision=lax.Precision.HIGHEST)
    column_norms = jnp.sqrt(lax.optimization_barrier(jnp.mean(transformed * transformed, axis=0)) + EPSILON)
    return (transformed / column_norms[None, :]).reshape(ZRB, N_PROW, BS, NRHS)
```

```python
import functools

import jax
import jax.numpy as jnp
from jax import lax
from jax.experimental import pallas as pl
from jax.experimental.pallas import tpu as pltpu
from jax.sharding import PartitionSpec as P

EPSILON = 1e-06
F32 = jnp.float32
BF16 = jnp.bfloat16


def split(x):
    high = x.astype(BF16)
    return high, (x - high.astype(F32)).astype(BF16)


def mm(a, b):
    return jnp.dot(a, b, preferred_element_type=F32)


def dot3(a, b):
    a_high, a_low = split(a)
    b_high, b_low = split(b)
    return mm(a_high, b_high) + (mm(a_high, b_low) + mm(a_low, b_high))


def peers_of(axis, size):
    me = lax.axis_index(axis)
    return me, [lax.rem(me + d, size) for d in range(1, size)]


def send_all(axis, size, source, target, send_sem, recv_sem):
    me, peers = peers_of(axis, size)
    copies = []
    for d, peer in enumerate(peers):
        copy = pltpu.make_async_remote_copy(
            src_ref=source(peer),
            dst_ref=target(d),
            send_sem=send_sem.at[d],
            recv_sem=recv_sem.at[d],
            device_id={axis: peer},
            device_id_type=pl.DeviceIdType.MESH,
        )
        copy.start()
        copies.append(copy)
    return copies


def reduce_scatter(axis, size, parts, landed, send_sem, recv_sem):
    me = lax.axis_index(axis)
    copies = send_all(axis, size, lambda peer: parts.at[peer], lambda d: landed.at[d], send_sem, recv_sem)
    total = parts[me]
    for d, copy in enumerate(copies):
        copy.wait_recv()
        total = total + landed[d]
    return total, copies


def all_gather(axis, size, whole, send_sem, recv_sem):
    me = lax.axis_index(axis)
    return send_all(axis, size, lambda peer: whole.at[me], lambda d: whole.at[me], send_sem, recv_sem)


def kernel(
    sizes,
    schur_ref, inverse_ref, coupling_ref, z_ref, targets_ref, flags_ref,
    out_ref,
    s_mem, m_mem, c_mem, z_mem, load_sem,
    a_parts, a_landed, a_whole, b_parts, b_landed, b_whole,
    c_parts, c_landed, c_whole, d_parts, d_landed, e_own, e_row, e_col,
    a_ss, a_rs, a_sg, a_rg, b_ss, b_rs, b_sg, b_rg,
    c_ss, c_rs, c_sg, c_rg, d_ss, d_rs, e_ss, e_rs, e_sg, e_rg,
):
    n_row, n_col, block, strip, window, count, z_blocks = sizes
    share = block // n_col
    barrier = pltpu.get_barrier_semaphore()
    row, row_peers = peers_of("prow", n_row)
    col, col_peers = peers_of("pcol", n_col)
    for peer in row_peers:
        pl.semaphore_signal(barrier, inc=1, device_id={"prow": peer}, device_id_type=pl.DeviceIdType.MESH)
    for peer in col_peers:
        pl.semaphore_signal(barrier, inc=1, device_id={"pcol": peer}, device_id_type=pl.DeviceIdType.MESH)
    loads = [
        pltpu.make_async_copy(coupling_ref, c_mem, load_sem.at[0]),
        pltpu.make_async_copy(inverse_ref, m_mem, load_sem.at[1]),
        pltpu.make_async_copy(schur_ref.at[pl.ds(0, 2 * strip)], s_mem, load_sem.at[2]),
        pltpu.make_async_copy(z_ref, z_mem, load_sem.at[3]),
    ]
    for load in loads:
        load.start()
    columns = lax.broadcasted_iota(jnp.int32, (window, count), 0)
    targets = targets_ref[...]
    selection = (columns == targets).astype(F32) + flags_ref[...].astype(F32) * (columns == targets + 1).astype(F32)
    selection = selection.astype(BF16)

    def right_side(panel):
        c_high, c_low = split(c_mem[pl.ds(panel * strip, strip), :])
        return -(mm(c_high, selection) + mm(c_low, selection))

    def apply_inverse(panel, residual):
        total = None
        for part in range(strip // block):
            piece = m_mem[pl.ds(panel * block * 2 + part, block, stride=2), :]
            term = dot3(piece, residual[part * block : (part + 1) * block])
            total = term if total is None else total + term
        return total

    loads[0].wait()
    side = right_side(1)
    loads[1].wait()
    applied = apply_inverse(1, side)
    a_parts[...] = applied.reshape(a_parts.shape)
    pl.semaphore_wait(barrier, n_row + n_col - 2)

    total, a_sent = reduce_scatter("prow", n_row, a_parts, a_landed, a_ss, a_rs)
    a_whole[row] = total
    a_gather = all_gather("prow", n_row, a_whole, a_sg, a_rg)
    side = right_side(0)
    loads[2].wait()
    loads[3].wait()
    for copy in a_gather:
        copy.wait_recv()
    later = a_whole[...].reshape(block, count)

    partial = dot3(s_mem[pl.ds(1, strip, stride=2), :], later)
    b_parts[...] = partial.reshape(b_parts.shape)
    total, b_sent = reduce_scatter("pcol", n_col, b_parts, b_landed, b_ss, b_rs)
    b_whole[col] = total
    b_gather = all_gather("pcol", n_col, b_whole, b_sg, b_rg)
    z_later = dot3(z_mem[pl.ds(1, z_blocks * block, stride=2), :], later)
    for copy in b_gather:
        copy.wait_recv()
    residual = side - b_whole[...].reshape(strip, count)

    applied = apply_inverse(0, residual)
    c_parts[...] = applied.reshape(c_parts.shape)
    total, c_sent = reduce_scatter("prow", n_row, c_parts, c_landed, c_ss, c_rs)
    c_whole[row] = total
    c_gather = all_gather("prow", n_row, c_whole, c_sg, c_rg)
    for copy in c_gather:
        copy.wait_recv()
    first = c_whole[...].reshape(block, count)

    transformed = z_later + dot3(z_mem[pl.ds(0, z_blocks * block, stride=2), :], first)
    for peer in range(n_col):
        for z_block in range(z_blocks):
            start = z_block * block + peer * share
            d_parts[peer, z_block] = transformed[start : start + share]
    owned, d_sent = reduce_scatter("pcol", n_col, d_parts, d_landed, d_ss, d_rs)
    squares = jnp.sum(jnp.sum(owned * owned, axis=0), axis=0, keepdims=True)
    e_own[0] = squares
    e_sent = send_all("prow", n_row, lambda peer: e_own.at[0], lambda d: e_row.at[d], e_ss, e_rs)
    for d, copy in enumerate(e_sent):
        copy.wait_recv()
        squares = squares + e_row[d]
    e_own[1] = squares
    e_gather = send_all("pcol", n_col, lambda peer: e_own.at[1], lambda d: e_col.at[d], e_sg, e_rg)
    for d, copy in enumerate(e_gather):
        copy.wait_recv()
        squares = squares + e_col[d]
    rows = z_blocks * block * n_row
    divisor = jnp.sqrt(squares / rows + EPSILON)
    out_ref[...] = owned / divisor[None]
    for copy in a_sent + a_gather + b_sent + b_gather + c_sent + c_gather + d_sent + e_sent + e_gather:
        copy.wait_send()


def shards(n_row, n_col, schur, panel_inverse, coupling, zslab, targets, pair_flags):
    block = schur.shape[2]
    strip = panel_inverse.shape[3] * block
    window = coupling.shape[3]
    count = targets.shape[0]
    z_blocks = zslab.shape[0]
    share = block // n_col
    sizes = (n_row, n_col, block, strip, window, count, z_blocks)
    flat = lambda x: x.reshape(-1, block)
    dma = lambda n: pltpu.SemaphoreType.DMA((n - 1,))
    row_sems = [dma(n_row)] * 4
    col_sems = [dma(n_col)] * 4

    def buffers(size, height):
        piece = (height // size, count)
        return [
            pltpu.VMEM((size,) + piece, F32),
            pltpu.VMEM((size - 1,) + piece, F32),
            pltpu.VMEM((size,) + piece, F32),
        ]

    anywhere = pl.BlockSpec(memory_space=pl.ANY)
    local = pl.BlockSpec(memory_space=pltpu.VMEM)
    out = pl.pallas_call(
        functools.partial(kernel, sizes),
        out_shape=jax.ShapeDtypeStruct((z_blocks, share, count), F32),
        in_specs=[anywhere] * 4 + [local] * 2,
        out_specs=local,
        scratch_shapes=[
            pltpu.VMEM((2 * strip, block), F32),
            pltpu.VMEM((panel_inverse.size // block, block), F32),
            pltpu.VMEM((coupling.size // window, window), F32),
            pltpu.VMEM((zslab.size // block, block), F32),
            pltpu.SemaphoreType.DMA((4,)),
        ]
        + buffers(n_row, block)
        + buffers(n_col, strip)
        + buffers(n_row, block)
        + [
            pltpu.VMEM((n_col, z_blocks, share, count), F32),
            pltpu.VMEM((n_col - 1, z_blocks, share, count), F32),
            pltpu.VMEM((2, 1, count), F32),
            pltpu.VMEM((n_row - 1, 1, count), F32),
            pltpu.VMEM((n_col - 1, 1, count), F32),
        ]
        + row_sems
        + col_sems
        + row_sems
        + [dma(n_col)] * 2
        + [dma(n_row)] * 2
        + [dma(n_col)] * 2,
        compiler_params=pltpu.CompilerParams(collective_id=0, has_side_effects=True, vmem_limit_bytes=60 * 1024 * 1024),
    )(
        flat(schur),
        flat(panel_inverse),
        coupling.reshape(-1, window),
        flat(zslab),
        targets.reshape(1, -1),
        pair_flags.reshape(1, -1),
    )
    return out.reshape(z_blocks, 1, share, count)


def solution(mesh):
    in_specs = (
        P(None, "prow", None, None, "pcol", None),
        P(None, "pcol", None, None, "prow", None),
        P(None, "prow", None, None),
        P(None, "prow", None, None, "pcol", None),
        P(),
        P(),
    )
    out_specs = P(None, "prow", "pcol", None)
    body = functools.partial(shards, mesh.shape["prow"], mesh.shape["pcol"])
    return jax.shard_map(body, mesh=mesh, in_specs=in_specs, out_specs=out_specs, check_vma=False)
```

```python
import functools

import jax
import jax.numpy as jnp
from jax import lax
from jax.experimental import pallas as pl
from jax.experimental.pallas import tpu as pltpu
from jax.sharding import PartitionSpec as P

EPSILON = 1e-06
F32 = jnp.float32
BF16 = jnp.bfloat16
DIRECT_LIMIT = 64


def split(x):
    high = x.astype(BF16)
    return high, (x - high.astype(F32)).astype(BF16)


def mm(a, b):
    return jnp.dot(a, b, preferred_element_type=F32)


def dot3(a, b):
    a_high, a_low = split(a)
    b_high, b_low = split(b)
    return mm(a_high, b_high) + (mm(a_high, b_low) + mm(a_low, b_high))


def peers_of(axis, size):
    me = lax.axis_index(axis)
    return me, [lax.rem(me + d, size) for d in range(1, size)]


def send_all(axis, size, source, target, send_sem, recv_sem):
    me, peers = peers_of(axis, size)
    copies = []
    for d, peer in enumerate(peers):
        copy = pltpu.make_async_remote_copy(
            src_ref=source(peer),
            dst_ref=target(d),
            send_sem=send_sem.at[d],
            recv_sem=recv_sem.at[d],
            device_id={axis: peer},
            device_id_type=pl.DeviceIdType.MESH,
        )
        copy.start()
        copies.append(copy)
    return copies


def reduce_scatter(axis, size, parts, landed, send_sem, recv_sem):
    me = lax.axis_index(axis)
    copies = send_all(axis, size, lambda peer: parts.at[peer], lambda d: landed.at[d], send_sem, recv_sem)
    total = parts[me]
    for d, copy in enumerate(copies):
        copy.wait_recv()
        total = total + landed[d]
    return total, copies


def all_gather(axis, size, whole, send_sem, recv_sem):
    me = lax.axis_index(axis)
    return send_all(axis, size, lambda peer: whole.at[me], lambda d: whole.at[me], send_sem, recv_sem)


def kernel(
    sizes,
    schur_ref, inverse_ref, coupling_ref, z_ref, targets_ref, flags_ref,
    out_ref,
    s_mem, m_mem, c_mem, z_mem, load_sem,
    a_own, a_landed, b_parts, b_landed, b_whole, c_own, c_landed,
    d_parts, d_pair, d_sum, d_landed, e_own, e_row, e_col,
    a_ss, a_rs, b_ss, b_rs, b_sg, b_rg, c_ss, c_rs,
    p_ss, p_rs, d_ss, d_rs, e_ss, e_rs, e_sg, e_rg,
):
    n_row, n_col, block, strip, window, count, z_blocks = sizes
    share = block // n_col
    barrier = pltpu.get_barrier_semaphore()
    row, row_peers = peers_of("prow", n_row)
    col, col_peers = peers_of("pcol", n_col)
    n_chip = n_col // 2
    direct = n_row * n_col <= DIRECT_LIMIT
    all_peers = [
        (lax.rem(row + i, n_row), lax.rem(col + j, n_col)) for i in range(n_row) for j in range(n_col) if i + j > 0
    ]
    greeted = all_peers if direct else [(peer, col) for peer in row_peers] + [(row, peer) for peer in col_peers]
    for peer in greeted:
        pl.semaphore_signal(barrier, inc=1, device_id=peer, device_id_type=pl.DeviceIdType.MESH)
    loads = [
        pltpu.make_async_copy(coupling_ref, c_mem, load_sem.at[0]),
        pltpu.make_async_copy(inverse_ref, m_mem, load_sem.at[1]),
        pltpu.make_async_copy(schur_ref.at[pl.ds(0, 2 * strip)], s_mem, load_sem.at[2]),
        pltpu.make_async_copy(z_ref, z_mem, load_sem.at[3]),
    ]
    for load in loads:
        load.start()
    columns = lax.broadcasted_iota(jnp.int32, (window, count), 0)
    targets = targets_ref[...]
    selection = (columns == targets).astype(F32) + flags_ref[...].astype(F32) * (columns == targets + 1).astype(F32)
    selection = selection.astype(BF16)

    def right_side(panel):
        c_high, c_low = split(c_mem[pl.ds(panel * strip, strip), :])
        return -(mm(c_high, selection) + mm(c_low, selection))

    def apply_inverse(panel, residual):
        total = None
        for part in range(strip // block):
            piece = m_mem[pl.ds(panel * block * 2 + part, block, stride=2), :]
            term = dot3(piece, residual[part * block : (part + 1) * block])
            total = term if total is None else total + term
        return total

    loads[0].wait()
    side = right_side(1)
    loads[1].wait()
    applied = apply_inverse(1, side)
    a_own[...] = applied
    pl.semaphore_wait(barrier, len(greeted))

    a_sent = send_all("prow", n_row, lambda peer: a_own, lambda d: a_landed.at[d], a_ss, a_rs)
    side = right_side(0)
    loads[2].wait()
    loads[3].wait()
    later = applied
    for d, copy in enumerate(a_sent):
        copy.wait_recv()
        later = later + a_landed[d]

    partial = dot3(s_mem[pl.ds(1, strip, stride=2), :], later)
    b_parts[...] = partial.reshape(b_parts.shape)
    total, b_sent = reduce_scatter("pcol", n_col, b_parts, b_landed, b_ss, b_rs)
    b_whole[col] = total
    b_gather = all_gather("pcol", n_col, b_whole, b_sg, b_rg)
    z_later = dot3(z_mem[pl.ds(1, z_blocks * block, stride=2), :], later)
    for copy in b_gather:
        copy.wait_recv()
    residual = side - b_whole[...].reshape(strip, count)

    applied = apply_inverse(0, residual)
    c_own[...] = applied
    c_sent = send_all("prow", n_row, lambda peer: c_own, lambda d: c_landed.at[d], c_ss, c_rs)
    first = applied
    for d, copy in enumerate(c_sent):
        copy.wait_recv()
        first = first + c_landed[d]

    transformed = z_later + dot3(z_mem[pl.ds(0, z_blocks * block, stride=2), :], first)
    for peer in range(n_col):
        for z_block in range(z_blocks):
            start = z_block * block + peer * share
            d_parts[peer % 2, peer // 2, z_block] = transformed[start : start + share]
    core, chip = lax.rem(col, 2), col // 2
    places = [lax.rem(chip + d, n_chip) for d in range(1, n_chip)] + [chip]
    pair_sent = []
    for d, place in enumerate(places):
        copy = pltpu.make_async_remote_copy(
            src_ref=d_parts.at[1 - core, place],
            dst_ref=d_pair.at[place],
            send_sem=p_ss.at[d],
            recv_sem=p_rs.at[place],
            device_id={"pcol": col + 1 - 2 * core},
            device_id_type=pl.DeviceIdType.MESH,
        )
        copy.start()
        pair_sent.append(copy)
    d_sent = []
    for d, place in enumerate(places):
        pltpu.make_async_remote_copy(
            src_ref=d_parts.at[1 - core, place],
            dst_ref=d_pair.at[place],
            send_sem=p_ss.at[d],
            recv_sem=p_rs.at[place],
            device_id={"pcol": col + 1 - 2 * core},
            device_id_type=pl.DeviceIdType.MESH,
        ).wait_recv()
        owned = d_parts[core, place] + d_pair[place]
        if d < n_chip - 1:
            d_sum[d] = owned
            copy = pltpu.make_async_remote_copy(
                src_ref=d_sum.at[d],
                dst_ref=d_landed.at[d],
                send_sem=d_ss.at[d],
                recv_sem=d_rs.at[d],
                device_id={"pcol": 2 * place + core},
                device_id_type=pl.DeviceIdType.MESH,
            )
            copy.start()
            d_sent.append(copy)
    for d, copy in enumerate(d_sent):
        copy.wait_recv()
        owned = owned + d_landed[d]
    squares = jnp.sum(jnp.sum(owned * owned, axis=0), axis=0, keepdims=True)
    e_own[0] = squares
    if direct:
        e_sent = []
        for d, peer in enumerate(all_peers):
            copy = pltpu.make_async_remote_copy(
                src_ref=e_own.at[0],
                dst_ref=e_col.at[d],
                send_sem=e_sg.at[d],
                recv_sem=e_rg.at[d],
                device_id=peer,
                device_id_type=pl.DeviceIdType.MESH,
            )
            copy.start()
            e_sent.append(copy)
        for copy in e_sent:
            copy.wait_recv()
        squares = squares + jnp.sum(e_col[...], axis=0)
        e_gather = []
    else:
        e_sent = send_all("prow", n_row, lambda peer: e_own.at[0], lambda d: e_row.at[d], e_ss, e_rs)
        for d, copy in enumerate(e_sent):
            copy.wait_recv()
            squares = squares + e_row[d]
        e_own[1] = squares
        e_gather = send_all("pcol", n_col, lambda peer: e_own.at[1], lambda d: e_col.at[d], e_sg, e_rg)
        for d, copy in enumerate(e_gather):
            copy.wait_recv()
            squares = squares + e_col[d]
    rows = z_blocks * block * n_row
    divisor = jnp.sqrt(squares / rows + EPSILON)
    out_ref[...] = owned / divisor[None]
    for copy in a_sent + b_sent + b_gather + c_sent + pair_sent + d_sent + e_sent + e_gather:
        copy.wait_send()


def shards(n_row, n_col, schur, panel_inverse, coupling, zslab, targets, pair_flags):
    block = schur.shape[2]
    strip = panel_inverse.shape[3] * block
    window = coupling.shape[3]
    count = targets.shape[0]
    z_blocks = zslab.shape[0]
    share = block // n_col
    sizes = (n_row, n_col, block, strip, window, count, z_blocks)
    flat = lambda x: x.reshape(-1, block)
    dma = lambda n: pltpu.SemaphoreType.DMA((n - 1,))
    n_chip = n_col // 2
    last = n_row * n_col if n_row * n_col <= DIRECT_LIMIT else n_col
    piece = (z_blocks, share, count)
    direct_buffers = [pltpu.VMEM((block, count), F32), pltpu.VMEM((n_row - 1, block, count), F32)]

    def buffers(size, height):
        rows = (height // size, count)
        return [
            pltpu.VMEM((size,) + rows, F32),
            pltpu.VMEM((size - 1,) + rows, F32),
            pltpu.VMEM((size,) + rows, F32),
        ]

    anywhere = pl.BlockSpec(memory_space=pl.ANY)
    local = pl.BlockSpec(memory_space=pltpu.VMEM)
    out = pl.pallas_call(
        functools.partial(kernel, sizes),
        out_shape=jax.ShapeDtypeStruct((z_blocks, share, count), F32),
        in_specs=[anywhere] * 4 + [local] * 2,
        out_specs=local,
        scratch_shapes=[
            pltpu.VMEM((2 * strip, block), F32),
            pltpu.VMEM((panel_inverse.size // block, block), F32),
            pltpu.VMEM((coupling.size // window, window), F32),
            pltpu.VMEM((zslab.size // block, block), F32),
            pltpu.SemaphoreType.DMA((4,)),
        ]
        + direct_buffers
        + buffers(n_col, strip)
        + direct_buffers
        + [
            pltpu.VMEM((2, n_chip) + piece, F32),
            pltpu.VMEM((n_chip,) + piece, F32),
            pltpu.VMEM((n_chip - 1,) + piece, F32),
            pltpu.VMEM((n_chip - 1,) + piece, F32),
            pltpu.VMEM((2, 1, count), F32),
            pltpu.VMEM((n_row - 1, 1, count), F32),
            pltpu.VMEM((last - 1, 1, count), F32),
        ]
        + [dma(n_row)] * 2
        + [dma(n_col)] * 4
        + [dma(n_row)] * 2
        + [dma(n_chip + 1)] * 2
        + [dma(n_chip)] * 2
        + [dma(n_row)] * 2
        + [dma(last)] * 2,
        compiler_params=pltpu.CompilerParams(collective_id=0, has_side_effects=True, vmem_limit_bytes=60 * 1024 * 1024),
    )(
        flat(schur),
        flat(panel_inverse),
        coupling.reshape(-1, window),
        flat(zslab),
        targets.reshape(1, -1),
        pair_flags.reshape(1, -1),
    )
    return out.reshape(z_blocks, 1, share, count)


def solution(mesh):
    in_specs = (
        P(None, "prow", None, None, "pcol", None),
        P(None, "pcol", None, None, "prow", None),
        P(None, "prow", None, None),
        P(None, "prow", None, None, "pcol", None),
        P(),
        P(),
    )
    out_specs = P(None, "prow", "pcol", None)
    body = functools.partial(shards, mesh.shape["prow"], mesh.shape["pcol"])
    return jax.shard_map(body, mesh=mesh, in_specs=in_specs, out_specs=out_specs, check_vma=False)
```

```python
import functools

import jax
import jax.numpy as jnp
from jax import lax
from jax.experimental import pallas as pl
from jax.experimental.pallas import tpu as pltpu
from jax.sharding import PartitionSpec as P

EPSILON = 1e-06
F32 = jnp.float32
BF16 = jnp.bfloat16
DIRECT_LIMIT = 64
VMEM_LIMIT = 67043328


def split(x):
    high = x.astype(BF16)
    return high, (x - high.astype(F32)).astype(BF16)


def mm(a, b):
    return jnp.dot(a, b, preferred_element_type=F32)


def dot3(a, b):
    a_high, a_low = split(a)
    b_high, b_low = split(b)
    return mm(a_high, b_high) + (mm(a_high, b_low) + mm(a_low, b_high))


def exclusive_or(number, mask):
    result, bit = 0, 1
    while bit <= mask:
        digit = lax.rem(number // bit, 2)
        result = result + bit * (1 - digit if mask & bit else digit)
        bit *= 2
    return result + number // bit * bit


def partners(number, size):
    if size & (size - 1):
        raise ValueError("axis size")
    return [exclusive_or(number, mask) for mask in reversed(range(1, size))]


def peers_of(axis, size):
    me = lax.axis_index(axis)
    return me, partners(me, size)


def send_all(axis, size, source, target, send_sem, recv_sem):
    me, peers = peers_of(axis, size)
    copies = []
    for d, peer in enumerate(peers):
        copy = pltpu.make_async_remote_copy(
            src_ref=source(peer),
            dst_ref=target(d),
            send_sem=send_sem.at[d],
            recv_sem=recv_sem.at[d],
            device_id={axis: peer},
            device_id_type=pl.DeviceIdType.MESH,
        )
        copy.start()
        copies.append(copy)
    return copies


def reduce_scatter(axis, size, parts, landed, send_sem, recv_sem):
    me = lax.axis_index(axis)
    copies = send_all(axis, size, lambda peer: parts.at[peer], lambda d: landed.at[d], send_sem, recv_sem)
    total = parts[me]
    for d, copy in enumerate(copies):
        copy.wait_recv()
        total = total + landed[d]
    return total, copies


def all_gather(axis, size, whole, send_sem, recv_sem):
    me = lax.axis_index(axis)
    return send_all(axis, size, lambda peer: whole.at[me], lambda d: whole.at[me], send_sem, recv_sem)


def kernel(
    sizes,
    schur_ref, inverse_ref, coupling_ref, z_ref, targets_ref, flags_ref,
    out_ref,
    s_mem, m_mem, c_mem, z_mem, t_mem, load_sem,
    a_own, a_landed, b_parts, b_landed, b_whole, c_own, c_landed,
    d_parts, d_pair, d_sum, d_landed, e_own, e_row, e_col,
    a_ss, a_rs, b_ss, b_rs, b_sg, b_rg, c_ss, c_rs,
    p_ss, p_rs, d_ss, d_rs, e_ss, e_rs, e_sg, e_rg,
):
    n_row, n_col, block, strip, window, count, z_blocks = sizes
    share = block // n_col
    barrier = pltpu.get_barrier_semaphore()
    row, row_peers = peers_of("prow", n_row)
    col, col_peers = peers_of("pcol", n_col)
    n_chip = n_col // 2
    direct = n_row * n_col <= DIRECT_LIMIT
    all_peers = [(i, j) for j in col_peers + [col] for i in row_peers + [row]][:-1]
    greeted = [(peer, col) for peer in row_peers] + [(row, peer) for peer in col_peers]
    for peer in greeted:
        pl.semaphore_signal(barrier, inc=1, device_id=peer, device_id_type=pl.DeviceIdType.MESH)
    loads = [
        pltpu.make_async_copy(targets_ref, t_mem.at[0], load_sem.at[4]),
        pltpu.make_async_copy(flags_ref, t_mem.at[1], load_sem.at[5]),
        pltpu.make_async_copy(coupling_ref, c_mem, load_sem.at[0]),
        pltpu.make_async_copy(inverse_ref, m_mem, load_sem.at[1]),
        pltpu.make_async_copy(schur_ref.at[pl.ds(0, 2 * strip)], s_mem, load_sem.at[2]),
        pltpu.make_async_copy(z_ref, z_mem, load_sem.at[3]),
    ]
    for load in loads:
        load.start()
    loads[0].wait()
    loads[1].wait()
    loads = loads[2:]
    columns = lax.broadcasted_iota(jnp.int32, (window, count), 0)
    targets = t_mem[0]
    selection = (columns == targets).astype(F32) + t_mem[1].astype(F32) * (columns == targets + 1).astype(F32)
    selection = selection.astype(BF16)

    def right_side(panel):
        c_high, c_low = split(c_mem[pl.ds(panel * strip, strip), :])
        return -(mm(c_high, selection) + mm(c_low, selection))

    def apply_inverse(panel, residual):
        total = None
        for part in range(strip // block):
            piece = m_mem[pl.ds(panel * block * 2 + part, block, stride=2), :]
            term = dot3(piece, residual[part * block : (part + 1) * block])
            total = term if total is None else total + term
        return total

    loads[0].wait()
    side = right_side(1)
    loads[1].wait()
    applied = apply_inverse(1, side)
    a_own[...] = applied
    pl.semaphore_wait(barrier, len(greeted))

    a_sent = send_all("prow", n_row, lambda peer: a_own, lambda d: a_landed.at[d], a_ss, a_rs)
    side = right_side(0)
    loads[2].wait()
    loads[3].wait()
    later = applied
    for d, copy in enumerate(a_sent):
        copy.wait_recv()
        later = later + a_landed[d]

    partial = dot3(s_mem[pl.ds(1, strip, stride=2), :], later)
    b_parts[...] = partial.reshape(b_parts.shape)
    total, b_sent = reduce_scatter("pcol", n_col, b_parts, b_landed, b_ss, b_rs)
    b_whole[col] = total
    b_gather = all_gather("pcol", n_col, b_whole, b_sg, b_rg)
    z_later = dot3(z_mem[pl.ds(1, z_blocks * block, stride=2), :], later)
    for copy in b_gather:
        copy.wait_recv()
    residual = side - b_whole[...].reshape(strip, count)

    applied = apply_inverse(0, residual)
    c_own[...] = applied
    c_sent = send_all("prow", n_row, lambda peer: c_own, lambda d: c_landed.at[d], c_ss, c_rs)
    first = applied
    for d, copy in enumerate(c_sent):
        copy.wait_recv()
        first = first + c_landed[d]

    transformed = z_later + dot3(z_mem[pl.ds(0, z_blocks * block, stride=2), :], first)
    for peer in range(n_col):
        for z_block in range(z_blocks):
            start = z_block * block + peer * share
            d_parts[peer % 2, peer // 2, z_block] = transformed[start : start + share]
    core, chip = lax.rem(col, 2), col // 2
    places = partners(chip, n_chip) + [chip]
    pair_sent = []
    for d, place in enumerate(places):
        copy = pltpu.make_async_remote_copy(
            src_ref=d_parts.at[1 - core, place],
            dst_ref=d_pair.at[place],
            send_sem=p_ss.at[d],
            recv_sem=p_rs.at[place],
            device_id={"pcol": col + 1 - 2 * core},
            device_id_type=pl.DeviceIdType.MESH,
        )
        copy.start()
        pair_sent.append(copy)
    d_sent = []
    for d, place in enumerate(places):
        pltpu.make_async_remote_copy(
            src_ref=d_parts.at[1 - core, place],
            dst_ref=d_pair.at[place],
            send_sem=p_ss.at[d],
            recv_sem=p_rs.at[place],
            device_id={"pcol": col + 1 - 2 * core},
            device_id_type=pl.DeviceIdType.MESH,
        ).wait_recv()
        owned = d_parts[core, place] + d_pair[place]
        if d < n_chip - 1:
            d_sum[d] = owned
            copy = pltpu.make_async_remote_copy(
                src_ref=d_sum.at[d],
                dst_ref=d_landed.at[d],
                send_sem=d_ss.at[d],
                recv_sem=d_rs.at[d],
                device_id={"pcol": 2 * place + core},
                device_id_type=pl.DeviceIdType.MESH,
            )
            copy.start()
            d_sent.append(copy)
    for d, copy in enumerate(d_sent):
        copy.wait_recv()
        owned = owned + d_landed[d]
    squares = jnp.sum(jnp.sum(owned * owned, axis=0), axis=0, keepdims=True)
    e_own[0] = squares
    if direct:
        e_sent = []
        for d, peer in enumerate(all_peers):
            copy = pltpu.make_async_remote_copy(
                src_ref=e_own.at[0],
                dst_ref=e_col.at[d],
                send_sem=e_sg.at[d],
                recv_sem=e_rg.at[d],
                device_id=peer,
                device_id_type=pl.DeviceIdType.MESH,
            )
            copy.start()
            e_sent.append(copy)
        for copy in e_sent:
            copy.wait_recv()
        squares = squares + jnp.sum(e_col[...], axis=0)
        e_gather = []
    else:
        e_sent = send_all("prow", n_row, lambda peer: e_own.at[0], lambda d: e_row.at[d], e_ss, e_rs)
        for d, copy in enumerate(e_sent):
            copy.wait_recv()
            squares = squares + e_row[d]
        e_own[1] = squares
        e_gather = send_all("pcol", n_col, lambda peer: e_own.at[1], lambda d: e_col.at[d], e_sg, e_rg)
        for d, copy in enumerate(e_gather):
            copy.wait_recv()
            squares = squares + e_col[d]
    out_ref[...] = owned / jnp.sqrt(squares / (z_blocks * block * n_row) + EPSILON)[None]
    for copy in a_sent + b_sent + b_gather + c_sent + pair_sent + d_sent + e_sent + e_gather:
        copy.wait_send()


def shards(n_row, n_col, schur, panel_inverse, coupling, zslab, targets, pair_flags):
    block = schur.shape[2]
    strip = panel_inverse.shape[3] * block
    window = coupling.shape[3]
    count = targets.shape[0]
    z_blocks = zslab.shape[0]
    share = block // n_col
    sizes = (n_row, n_col, block, strip, window, count, z_blocks)
    flat = lambda x: x.reshape(-1, block)
    dma = lambda n: pltpu.SemaphoreType.DMA((n - 1,))
    n_chip = n_col // 2
    last = n_row * n_col if n_row * n_col <= DIRECT_LIMIT else n_col
    piece = (z_blocks, share, count)
    direct_buffers = [pltpu.VMEM((block, count), F32), pltpu.VMEM((n_row - 1, block, count), F32)]

    def buffers(size, height):
        rows = (height // size, count)
        return [
            pltpu.VMEM((size,) + rows, F32),
            pltpu.VMEM((size - 1,) + rows, F32),
            pltpu.VMEM((size,) + rows, F32),
        ]

    anywhere = pl.BlockSpec(memory_space=pl.ANY)
    local = pl.BlockSpec(memory_space=pltpu.VMEM)
    out = pl.pallas_call(
        functools.partial(kernel, sizes),
        out_shape=jax.ShapeDtypeStruct(piece, F32),
        in_specs=[anywhere] * 6,
        out_specs=local,
        scratch_shapes=[
            pltpu.VMEM((2 * strip, block), F32),
            pltpu.VMEM((panel_inverse.size // block, block), F32),
            pltpu.VMEM((coupling.size // window, window), F32),
            pltpu.VMEM((zslab.size // block, block), F32),
            pltpu.VMEM((2, 1, count), jnp.int32),
            pltpu.SemaphoreType.DMA((6,)),
        ]
        + direct_buffers
        + buffers(n_col, strip)
        + direct_buffers
        + [
            pltpu.VMEM((2, n_chip) + piece, F32),
            pltpu.VMEM((n_chip,) + piece, F32),
            pltpu.VMEM((n_chip - 1,) + piece, F32),
            pltpu.VMEM((n_chip - 1,) + piece, F32),
            pltpu.VMEM((2, 1, count), F32),
            pltpu.VMEM((n_row - 1, 1, count), F32),
            pltpu.VMEM((last - 1, 1, count), F32),
        ]
        + [dma(n_row)] * 2
        + [dma(n_col)] * 4
        + [dma(n_row)] * 2
        + [dma(n_chip + 1)] * 2
        + [dma(n_chip)] * 2
        + [dma(n_row)] * 2
        + [dma(last)] * 2,
        compiler_params=pltpu.CompilerParams(collective_id=0, has_side_effects=True, vmem_limit_bytes=VMEM_LIMIT),
    )(
        flat(schur),
        flat(panel_inverse),
        coupling.reshape(-1, window),
        flat(zslab),
        targets.reshape(1, -1),
        pair_flags.reshape(1, -1),
    )
    return out.reshape(z_blocks, 1, share, count)


def solution(mesh):
    in_specs = (
        P(None, "prow", None, None, "pcol", None),
        P(None, "pcol", None, None, "prow", None),
        P(None, "prow", None, None),
        P(None, "prow", None, None, "pcol", None),
        P(),
        P(),
    )
    out_specs = P(None, "prow", "pcol", None)
    body = functools.partial(shards, mesh.shape["prow"], mesh.shape["pcol"])
    return jax.shard_map(body, mesh=mesh, in_specs=in_specs, out_specs=out_specs, check_vma=False)
```

```python
import functools

import jax
import jax.numpy as jnp
from jax import lax
from jax.experimental import pallas as pl
from jax.experimental.pallas import tpu as pltpu
from jax.sharding import PartitionSpec as P

EPSILON = 1e-06
F32 = jnp.float32
BF16 = jnp.bfloat16
DIRECT_LIMIT = 64
VMEM_LIMIT = 67043328


def split(x):
    high = x.astype(BF16)
    return high, (x - high.astype(F32)).astype(BF16)


def mm(a, b):
    return jnp.dot(a, b, preferred_element_type=F32)


def dot3(a, b):
    a_high, a_low = split(a)
    b_high, b_low = split(b)
    return mm(a_high, b_high) + (mm(a_high, b_low) + mm(a_low, b_high))


def exclusive_or(number, mask):
    result, bit = 0, 1
    while bit <= mask:
        digit = lax.rem(number // bit, 2)
        result = result + bit * (1 - digit if mask & bit else digit)
        bit *= 2
    return result + number // bit * bit


def partners(number, size):
    if size & (size - 1):
        raise ValueError("axis size")
    return [exclusive_or(number, mask) for mask in reversed(range(1, size))]


def peers_of(axis, size):
    me = lax.axis_index(axis)
    return me, partners(me, size)


def send_all(axis, size, source, target, send_sem, recv_sem):
    me, peers = peers_of(axis, size)
    copies = []
    for d, peer in enumerate(peers):
        copy = pltpu.make_async_remote_copy(
            src_ref=source(peer),
            dst_ref=target(d),
            send_sem=send_sem.at[d],
            recv_sem=recv_sem.at[d],
            device_id={axis: peer},
            device_id_type=pl.DeviceIdType.MESH,
        )
        copy.start()
        copies.append(copy)
    return copies


def reduce_scatter(axis, size, parts, landed, send_sem, recv_sem):
    me = lax.axis_index(axis)
    copies = send_all(axis, size, lambda peer: parts.at[peer], lambda d: landed.at[d], send_sem, recv_sem)
    total = parts[me]
    for d, copy in enumerate(copies):
        copy.wait_recv()
        total = total + landed[d]
    return total, copies


def all_gather(axis, size, whole, send_sem, recv_sem):
    me = lax.axis_index(axis)
    return send_all(axis, size, lambda peer: whole.at[me], lambda d: whole.at[me], send_sem, recv_sem)


def kernel(
    sizes,
    schur_ref, inverse_ref, coupling_ref, z_ref, targets_ref, flags_ref,
    out_ref,
    s_mem, m_mem, c_mem, z_mem, t_mem, load_sem, relay_sem,
    a_own, a_landed, b_parts, b_landed, b_whole, c_own, c_landed,
    d_parts, d_pair, d_sum, d_landed, e_own, e_row, e_col,
    a_ss, a_rs, b_ss, b_rs, b_sg, b_rg, c_ss, c_rs,
    p_ss, p_rs, d_ss, d_rs, e_ss, e_rs, e_sg, e_rg,
):
    n_row, n_col, block, strip, window, count, z_blocks = sizes
    share = block // n_col
    barrier = pltpu.get_barrier_semaphore()
    row, row_peers = peers_of("prow", n_row)
    col, col_peers = peers_of("pcol", n_col)
    n_chip = n_col // 2
    direct = n_row * n_col <= DIRECT_LIMIT
    all_peers = [(i, j) for j in col_peers + [col] for i in row_peers + [row]][:-1]
    core, chip = lax.rem(col, 2), col // 2

    def greet(semaphore, reach):
        near = 1
        pl.semaphore_signal(
            semaphore, inc=1, device_id={"pcol": col + 1 - 2 * core}, device_id_type=pl.DeviceIdType.MESH
        )
        for step in range(-min(reach, n_chip - 1), min(reach, n_chip - 1) + 1):
            if step:
                place = chip + step
                inside = jnp.logical_and(place >= 0, place < n_chip)

                @pl.when(inside)
                def _():
                    for other in range(2):
                        pl.semaphore_signal(
                            semaphore,
                            inc=1,
                            device_id={"pcol": 2 * place + other},
                            device_id_type=pl.DeviceIdType.MESH,
                        )

                near = near + jnp.where(inside, 2, 0)
        return near

    for peer in row_peers:
        pl.semaphore_signal(barrier, inc=1, device_id={"prow": peer}, device_id_type=pl.DeviceIdType.MESH)
    near = greet(barrier, 1)
    loads = [
        pltpu.make_async_copy(targets_ref, t_mem.at[0], load_sem.at[4]),
        pltpu.make_async_copy(flags_ref, t_mem.at[1], load_sem.at[5]),
        pltpu.make_async_copy(coupling_ref, c_mem, load_sem.at[0]),
        pltpu.make_async_copy(inverse_ref, m_mem, load_sem.at[1]),
        pltpu.make_async_copy(schur_ref.at[pl.ds(0, 2 * strip)], s_mem, load_sem.at[2]),
        pltpu.make_async_copy(z_ref, z_mem, load_sem.at[3]),
    ]
    for load in loads:
        load.start()
    loads[0].wait()
    loads[1].wait()
    loads = loads[2:]
    columns = lax.broadcasted_iota(jnp.int32, (window, count), 0)
    targets = t_mem[0]
    selection = (columns == targets).astype(F32) + t_mem[1].astype(F32) * (columns == targets + 1).astype(F32)
    selection = selection.astype(BF16)

    def right_side(panel):
        c_high, c_low = split(c_mem[pl.ds(panel * strip, strip), :])
        return -(mm(c_high, selection) + mm(c_low, selection))

    def apply_inverse(panel, residual):
        total = None
        for part in range(strip // block):
            piece = m_mem[pl.ds(panel * block * 2 + part, block, stride=2), :]
            term = dot3(piece, residual[part * block : (part + 1) * block])
            total = term if total is None else total + term
        return total

    loads[0].wait()
    side = right_side(1)
    loads[1].wait()
    applied = apply_inverse(1, side)
    a_own[...] = applied
    pl.semaphore_wait(barrier, n_row - 1 + near)

    a_sent = send_all("prow", n_row, lambda peer: a_own, lambda d: a_landed.at[d], a_ss, a_rs)
    side = right_side(0)
    for index in range((n_chip - 1).bit_length()):
        pl.semaphore_wait(relay_sem.at[index], greet(relay_sem.at[index], 2**index))
    loads[2].wait()
    loads[3].wait()
    later = applied
    for d, copy in enumerate(a_sent):
        copy.wait_recv()
        later = later + a_landed[d]

    partial = dot3(s_mem[pl.ds(1, strip, stride=2), :], later)
    b_parts[...] = partial.reshape(b_parts.shape)
    total, b_sent = reduce_scatter("pcol", n_col, b_parts, b_landed, b_ss, b_rs)
    b_whole[col] = total
    b_gather = all_gather("pcol", n_col, b_whole, b_sg, b_rg)
    z_later = dot3(z_mem[pl.ds(1, z_blocks * block, stride=2), :], later)
    for copy in b_gather:
        copy.wait_recv()
    residual = side - b_whole[...].reshape(strip, count)

    applied = apply_inverse(0, residual)
    c_own[...] = applied
    c_sent = send_all("prow", n_row, lambda peer: c_own, lambda d: c_landed.at[d], c_ss, c_rs)
    first = applied
    for d, copy in enumerate(c_sent):
        copy.wait_recv()
        first = first + c_landed[d]

    transformed = z_later + dot3(z_mem[pl.ds(0, z_blocks * block, stride=2), :], first)
    for peer in range(n_col):
        for z_block in range(z_blocks):
            start = z_block * block + peer * share
            d_parts[peer % 2, peer // 2, z_block] = transformed[start : start + share]
    core, chip = lax.rem(col, 2), col // 2
    places = partners(chip, n_chip) + [chip]
    pair_sent = []
    for d, place in enumerate(places):
        copy = pltpu.make_async_remote_copy(
            src_ref=d_parts.at[1 - core, place],
            dst_ref=d_pair.at[place],
            send_sem=p_ss.at[d],
            recv_sem=p_rs.at[place],
            device_id={"pcol": col + 1 - 2 * core},
            device_id_type=pl.DeviceIdType.MESH,
        )
        copy.start()
        pair_sent.append(copy)
    d_sent = []
    for d, place in enumerate(places):
        pltpu.make_async_remote_copy(
            src_ref=d_parts.at[1 - core, place],
            dst_ref=d_pair.at[place],
            send_sem=p_ss.at[d],
            recv_sem=p_rs.at[place],
            device_id={"pcol": col + 1 - 2 * core},
            device_id_type=pl.DeviceIdType.MESH,
        ).wait_recv()
        owned = d_parts[core, place] + d_pair[place]
        if d < n_chip - 1:
            d_sum[d] = owned
            copy = pltpu.make_async_remote_copy(
                src_ref=d_sum.at[d],
                dst_ref=d_landed.at[d],
                send_sem=d_ss.at[d],
                recv_sem=d_rs.at[d],
                device_id={"pcol": 2 * place + core},
                device_id_type=pl.DeviceIdType.MESH,
            )
            copy.start()
            d_sent.append(copy)
    for d, copy in enumerate(d_sent):
        copy.wait_recv()
        owned = owned + d_landed[d]
    squares = jnp.sum(jnp.sum(owned * owned, axis=0), axis=0, keepdims=True)
    e_own[0] = squares
    if direct:
        e_sent = []
        for d, peer in enumerate(all_peers):
            copy = pltpu.make_async_remote_copy(
                src_ref=e_own.at[0],
                dst_ref=e_col.at[d],
                send_sem=e_sg.at[d],
                recv_sem=e_rg.at[d],
                device_id=peer,
                device_id_type=pl.DeviceIdType.MESH,
            )
            copy.start()
            e_sent.append(copy)
        for copy in e_sent:
            copy.wait_recv()
        squares = squares + jnp.sum(e_col[...], axis=0)
        e_gather = []
    else:
        e_sent = send_all("prow", n_row, lambda peer: e_own.at[0], lambda d: e_row.at[d], e_ss, e_rs)
        for d, copy in enumerate(e_sent):
            copy.wait_recv()
            squares = squares + e_row[d]
        e_own[1] = squares
        e_gather = send_all("pcol", n_col, lambda peer: e_own.at[1], lambda d: e_col.at[d], e_sg, e_rg)
        for d, copy in enumerate(e_gather):
            copy.wait_recv()
            squares = squares + e_col[d]
    out_ref[...] = owned / jnp.sqrt(squares / (z_blocks * block * n_row) + EPSILON)[None]
    for copy in a_sent + b_sent + b_gather + c_sent + pair_sent + d_sent + e_sent + e_gather:
        copy.wait_send()


def shards(n_row, n_col, schur, panel_inverse, coupling, zslab, targets, pair_flags):
    block = schur.shape[2]
    strip = panel_inverse.shape[3] * block
    window = coupling.shape[3]
    count = targets.shape[0]
    z_blocks = zslab.shape[0]
    share = block // n_col
    sizes = (n_row, n_col, block, strip, window, count, z_blocks)
    flat = lambda x: x.reshape(-1, block)
    dma = lambda n: pltpu.SemaphoreType.DMA((n - 1,))
    n_chip = n_col // 2
    last = n_row * n_col if n_row * n_col <= DIRECT_LIMIT else n_col
    piece = (z_blocks, share, count)
    direct_buffers = [pltpu.VMEM((block, count), F32), pltpu.VMEM((n_row - 1, block, count), F32)]

    def buffers(size, height):
        rows = (height // size, count)
        return [
            pltpu.VMEM((size,) + rows, F32),
            pltpu.VMEM((size - 1,) + rows, F32),
            pltpu.VMEM((size,) + rows, F32),
        ]

    anywhere = pl.BlockSpec(memory_space=pl.ANY)
    local = pl.BlockSpec(memory_space=pltpu.VMEM)
    out = pl.pallas_call(
        functools.partial(kernel, sizes),
        out_shape=jax.ShapeDtypeStruct(piece, F32),
        in_specs=[anywhere] * 6,
        out_specs=local,
        scratch_shapes=[
            pltpu.VMEM((2 * strip, block), F32),
            pltpu.VMEM((panel_inverse.size // block, block), F32),
            pltpu.VMEM((coupling.size // window, window), F32),
            pltpu.VMEM((zslab.size // block, block), F32),
            pltpu.VMEM((2, 1, count), jnp.int32),
            pltpu.SemaphoreType.DMA((6,)),
            pltpu.SemaphoreType.REGULAR((max((n_chip - 1).bit_length(), 1),)),
        ]
        + direct_buffers
        + buffers(n_col, strip)
        + direct_buffers
        + [
            pltpu.VMEM((2, n_chip) + piece, F32),
            pltpu.VMEM((n_chip,) + piece, F32),
            pltpu.VMEM((n_chip - 1,) + piece, F32),
            pltpu.VMEM((n_chip - 1,) + piece, F32),
            pltpu.VMEM((2, 1, count), F32),
            pltpu.VMEM((n_row - 1, 1, count), F32),
            pltpu.VMEM((last - 1, 1, count), F32),
        ]
        + [dma(n_row)] * 2
        + [dma(n_col)] * 4
        + [dma(n_row)] * 2
        + [dma(n_chip + 1)] * 2
        + [dma(n_chip)] * 2
        + [dma(n_row)] * 2
        + [dma(last)] * 2,
        compiler_params=pltpu.CompilerParams(collective_id=0, has_side_effects=True, vmem_limit_bytes=VMEM_LIMIT),
    )(
        flat(schur),
        flat(panel_inverse),
        coupling.reshape(-1, window),
        flat(zslab),
        targets.reshape(1, -1),
        pair_flags.reshape(1, -1),
    )
    return out.reshape(z_blocks, 1, share, count)


def solution(mesh):
    in_specs = (
        P(None, "prow", None, None, "pcol", None),
        P(None, "pcol", None, None, "prow", None),
        P(None, "prow", None, None),
        P(None, "prow", None, None, "pcol", None),
        P(),
        P(),
    )
    out_specs = P(None, "prow", "pcol", None)
    body = functools.partial(shards, mesh.shape["prow"], mesh.shape["pcol"])
    return jax.shard_map(body, mesh=mesh, in_specs=in_specs, out_specs=out_specs, check_vma=False)
```
